32 devices in a mesh: group: 4 (over x, core), shard: 8 (over z, y).
Axes of the slice: x: 2, y: 2, z: 4, core: 2. Of those that a mesh axis runs over, the one named last changes fastest.
Arguments:
- step_index: int32 [1], replicated, may hold values from 0 to 1023
- hidden: bfloat16 [4, 8192, 4608], P('group', 'shard'), may hold values from -600 to 600
- upstream: bfloat16 [4, 8192, 2304], P('group', 'shard'), may hold values from -40 to 40
- numerator: float32 [4, 4608, 2304], P('group', 'shard'), may hold values from -6 to 6
- push_weight: float32 [4], P('group'), may hold values from 0.5 to 2
Outputs:
- numerator_next: float32 [4, 4608, 2304], P('group', 'shard')
- weight_next: float32 [4], P('group')
- params: bfloat16 [4, 4608, 2304], P('group', 'shard')
The draws below stay inside these ranges and needn't reach their ends.
All inputs are finite; a program needn't handle non-finite values.
Results may differ from the reference program's by a relative error of at most 0.009.
Values may be sent and summed in bfloat16 or wider, within the bound.
No kernel may reach another device: no remote copies, remote signals or barrier semaphores. Data moves between devices by JAX's collectives and lax.ppermute only.
A program may use at most 128 MiB of HBM per device.

```python
import math
import jax
import jax.numpy as jnp
from jax import lax

D = 2304
FF = 4608
TOK_DEV = 1024
GROUPS = 4
SHARDS = 8
TOK_GROUP = 8192


def draw_hidden(key, part):
    keys = jax.random.split(key, 4)
    position = jnp.arange(FF, dtype=jnp.float32)
    column_scale = 10.0 ** jax.random.uniform(keys[0], (FF,), jnp.float32) * 3.0 ** (position / FF) / 4.0
    row_scale = 10.0 ** jax.random.uniform(keys[1], (GROUPS, TOK_GROUP, 1), jnp.float32) / 4.0
    owner = jax.random.permutation(keys[2], SHARDS)
    token_block = jnp.arange(TOK_GROUP) // TOK_DEV
    unit_block = jnp.arange(FF) // (FF // SHARDS)
    spike = jnp.where(owner[token_block][:, None] == unit_block[None, :], 3.0, 1.0)
    shape = (GROUPS, TOK_GROUP, FF)
    base = jnp.clip(jax.random.normal(keys[3], shape, jnp.float32), -5.0, 5.0)
    return (base * row_scale * column_scale * spike).astype(jnp.bfloat16)


def draw_upstream(key, part):
    keys = jax.random.split(key, 2)
    column_scale = 10.0 ** jax.random.uniform(keys[0], (D,), jnp.float32) / 3.0
    shape = (GROUPS, TOK_GROUP, D)
    base = jnp.clip(jax.random.normal(keys[1], shape, jnp.float32), -5.0, 5.0)
    return (base * column_scale).astype(jnp.bfloat16)


def steps_of(stream_key, shape, shards, smallest, high):
    gain, own = 1.0, jax.random.fold_in(stream_key, 6)
    for axis_at, parts in shards:
        heights = jnp.exp(jax.random.uniform(jax.random.fold_in(own, axis_at), (parts,), jnp.float32, smallest / len(shards), high / len(shards)))
        gain = gain * jnp.repeat(heights, shape[axis_at] // parts).reshape([-1 if axis == axis_at else 1 for axis in range(len(shape))])
    return gain


def scatter_about(own_key, dims, scale, bound, cuts=(), held_as=jnp.bfloat16):
    level = steps_of(own_key, dims, cuts, -0.22, 0.18) if cuts else 1.0
    result = jax.random.normal(own_key, dims, jnp.float32) * scale * level
    return jnp.minimum(jnp.maximum(result, -bound), bound).astype(held_as)


def setup_inputs(seed: int = 0) -> dict:
    splits = jax.random.split(jax.random.key(seed), 6)
    return {
        "step_index": jax.random.randint(splits[0], (1,), 0, 1024).astype(jnp.int32),
        "hidden": draw_hidden(jax.random.fold_in(splits[5], 71), 0),
        "upstream": draw_upstream(jax.random.fold_in(splits[5], 71), 0),
        "numerator": scatter_about(splits[3], (GROUPS, FF, D), 1.0, 6.0, ((0, 4), (1, 8)), jnp.float32),
        "push_weight": jnp.clip(jnp.exp(math.log(2.0) - 1.3862944 * jax.random.uniform(splits[4], (GROUPS,), jnp.float32) ** steps_of(splits[4], (GROUPS,), ((0, 4),), -0.2, 0.2)), 0.5, 2.0),
    }


learning_rate = 0.3
decay_steps = 256.0
clip_ceiling = 1.0
epsilon = 1e-06

def shard_gradient(hidden_rows, upstream_rows):
    hidden_blocks = hidden_rows.reshape(SHARDS, TOK_DEV, FF)
    upstream_blocks = upstream_rows.reshape(SHARDS, TOK_DEV, D)

    def accumulate(running, shard_pair):
        product = jnp.dot(shard_pair[0].astype(jnp.float32).T, shard_pair[1].astype(jnp.float32), preferred_element_type=jnp.float32, precision=lax.Precision.HIGHEST)
        rounded = lax.optimization_barrier(product.astype(jnp.bfloat16))
        return (running + rounded.astype(jnp.float32), None)
    summed, unused = lax.scan(accumulate, jnp.zeros((FF, D), jnp.float32), (hidden_blocks, upstream_blocks))
    return summed

def group_pair(arrays):
    return shard_gradient(arrays[0], arrays[1])

def reference(step_index, hidden, upstream, numerator, push_weight):
    gradient = lax.map(group_pair, (hidden, upstream))
    square_mean = lax.optimization_barrier(jnp.sum(gradient * gradient, axis=(1, 2))) / (FF * D)
    rate = learning_rate / jnp.sqrt(1.0 + step_index[0].astype(jnp.float32) / decay_steps)
    factor = rate * jnp.minimum(1.0, clip_ceiling / jnp.sqrt(square_mean + epsilon))
    pushed = numerator - factor[:, None, None] * gradient
    level_count = GROUPS.bit_length() - 1
    exponent = (step_index[0] % level_count).astype(jnp.int32)
    offset = jnp.left_shift(jnp.int32(1), exponent)
    peer_state = jnp.roll(pushed, offset, axis=0)
    peer_weight = jnp.roll(push_weight, offset, axis=0)
    numerator_next = 0.5 * (pushed + peer_state)
    weight_next = 0.5 * (push_weight + peer_weight)
    params = (numerator_next / weight_next[:, None, None]).astype(jnp.bfloat16)
    return (numerator_next, weight_next, params)
```

```python
from functools import partial

import jax
import jax.numpy as jnp
from jax import lax
from jax.sharding import PartitionSpec as P

learning_rate = 0.3
decay_steps = 256.0
clip_ceiling = 1.0
epsilon = 1e-06


outer_first_shares = (2, 1, 1, 0)
inner_first_shares = (3, 4, 4, 3)


def grid_of(count):
    outer = 1
    while outer * outer < count:
        outer *= 2
    while count % outer:
        outer += 1
    return outer, count // outer


def column_pieces(width):
    lane = 128
    unit = lane if width % lane == 0 else 1
    units = width // unit
    total = sum(outer_first_shares) + sum(inner_first_shares)
    pieces, start, seen = [], 0, 0
    for pair in zip(outer_first_shares, inner_first_shares):
        row = []
        for share in pair:
            seen += share
            end = (seen * units // total) * unit
            row.append((start, end) if end > start else None)
            start = end
        pieces.append(row)
    return pieces


def hop(x, outer, inner, outer_by, inner_by):
    pairs = [
        (o * inner + i, ((o + outer_by) % outer) * inner + (i + inner_by) % inner)
        for o in range(outer)
        for i in range(inner)
    ]
    return lax.ppermute(x, "shard", pairs)


def ring_sums(rings, count):
    sums = [block(position - way) for block, position, way, send in rings]
    for step in range(count - 1):
        arrived = [send(s.astype(jnp.bfloat16)) for s, (block, position, way, send) in zip(sums, rings)]
        sums = [
            a.astype(jnp.float32) + block(position - way * (step + 2)).astype(jnp.float32)
            for a, (block, position, way, send) in zip(arrived, rings)
        ]
    return sums


def outer_rings(blocks, outer, inner, at):
    half = blocks.shape[1] // 2

    def getter(low, high):
        return lambda j: lax.dynamic_index_in_dim(blocks, j % outer, 0, keepdims=False)[low:high]

    rings = [
        (getter(0, half), at, 1, lambda x: hop(x, outer, inner, 1, 0)),
        (getter(half, blocks.shape[1]), at, -1, lambda x: hop(x, outer, inner, -1, 0)),
    ]
    return jnp.concatenate(ring_sums(rings, outer), axis=0)


def inner_ring(blocks, outer, inner, at):
    axis = blocks.ndim - 3
    ring = (
        lambda j: lax.dynamic_index_in_dim(blocks, j % inner, axis, keepdims=False),
        at,
        1,
        lambda x: hop(x, outer, inner, 0, 1),
    )
    return ring_sums([ring], inner)[0]


def step_with(exponent, step_index, own_hidden, own_upstream, own_state, push_weight):
    groups, shards_count = lax.axis_size("group"), lax.axis_size("shard")
    outer, inner = grid_of(shards_count)
    shard = lax.axis_index("shard")
    group = lax.axis_index("group")
    outer_at, inner_at = shard // inner, shard % inner
    rows, width = own_state.shape
    entry_count = rows * shards_count * width
    offset = 1 << exponent
    gossip = [(i, (i + offset) % groups) for i in range(groups)]

    def product(span):
        part = lax.dot_general(
            own_hidden, own_upstream[:, span[0]:span[1]], (((0,), (0,)), ((), ())),
            preferred_element_type=jnp.float32,
        )
        return part.astype(jnp.bfloat16)

    peer_state = lax.ppermute(own_state.astype(jnp.bfloat16), "group", gossip)

    pieces = column_pieces(width)
    own_parts, peer_parts, square = {}, {}, 0.0
    after_outer, after_inner = None, None
    for stage in range(len(pieces) + 1):
        first, second = pieces[stage] if stage < len(pieces) else (None, None)
        fresh = tuple(None if span is None else product(span) for span in (first, second))
        (to_outer, to_inner), from_outer, from_inner = lax.optimization_barrier(
            (fresh, after_outer, after_inner)
        )
        after_outer, after_inner, done = None, None, {}
        if to_inner is not None:
            after_inner = inner_ring(to_inner.reshape(outer, inner, rows, -1), outer, inner, inner_at)
        if from_outer is not None:
            done[pieces[stage - 1][0]] = inner_ring(
                from_outer.reshape(inner, rows, -1), outer, inner, inner_at
            )
        if from_inner is not None:
            done[pieces[stage - 1][1]] = outer_rings(from_inner, outer, inner, outer_at)
        if to_outer is not None:
            after_outer = outer_rings(
                to_outer.reshape(outer, inner * rows, -1), outer, inner, outer_at
            )
        if done:
            spans = sorted(done)
            grad = jnp.concatenate([done[span] for span in spans], axis=1)
            square = square + jnp.sum(grad * grad)
            own_parts[spans[0]] = grad
            peer_parts[spans[0]] = lax.ppermute(grad.astype(jnp.bfloat16), "group", gossip)

    here = jnp.arange(groups) == group
    totals = lax.psum(
        jnp.concatenate([
            jnp.where(here, square, 0.0),
            jnp.where(here & (shard == 0), push_weight[0], 0.0),
        ]),
        ("group", "shard"),
    )
    rate = learning_rate / jnp.sqrt(1.0 + step_index[0].astype(jnp.float32) / decay_steps)
    factors = rate * jnp.minimum(1.0, clip_ceiling / jnp.sqrt(totals[:groups] / entry_count + epsilon))
    weights = totals[groups:]
    peer = (group - offset) % groups
    own_factor, peer_factor = factors[group], factors[peer]
    weight_next = 0.5 * (push_weight + weights[peer])
    own_grad = jnp.concatenate([own_parts[span] for span in sorted(own_parts)], axis=1)
    peer_grad = jnp.concatenate([peer_parts[span] for span in sorted(peer_parts)], axis=1).astype(jnp.float32)
    mixed = 0.5 * (
        (own_state - own_factor * own_grad)
        + (peer_state.astype(jnp.float32) - peer_factor * peer_grad)
    )
    return mixed, weight_next, (mixed / weight_next[0]).astype(jnp.bfloat16)


def shards(step_index, hidden, upstream, numerator, push_weight):
    level_count = lax.axis_size("group").bit_length() - 1
    branches = [partial(step_with, exponent) for exponent in range(level_count)]
    mixed, weight_next, params = lax.switch(
        step_index[0] % level_count, branches,
        step_index, hidden[0], upstream[0], numerator[0], push_weight,
    )
    return mixed[None], weight_next, params[None]


def solution(mesh):
    placed = (
        P(),
        P("group", "shard", None),
        P("group", "shard", None),
        P("group", "shard", None),
        P("group"),
    )
    return jax.shard_map(
        shards,
        mesh=mesh,
        in_specs=placed,
        out_specs=(P("group", "shard", None), P("group"), P("group", "shard", None)),
        check_vma=False,
    )
```
